32 devices in a mesh: boxx: 4 (over y, core), boxyz: 8 (over z, x).
Axes of the slice: x: 2, y: 2, z: 4, core: 2. Of those that a mesh axis runs over, the one named last changes fastest.
Arguments:
- face_block: bfloat16 [4, 4, 64, 256, 256], P('boxx', None, 'boxyz'), may hold values from -0.375 to 0.375
- couple_minus: bfloat16 [4, 4, 64, 256, 256], P('boxx', None, 'boxyz'), may hold values from -0.375 to 0.375
- couple_plus: bfloat16 [4, 4, 64, 256, 256], P('boxx', None, 'boxyz'), may hold values from -0.375 to 0.375
- couple_up: bfloat16 [4, 4, 64, 256, 256], P('boxx', None, 'boxyz'), may hold values from -0.375 to 0.375
- interp: bfloat16 [4, 4, 64, 256, 128], P('boxx', None, 'boxyz'), may hold values from -0.5 to 0.5
- pivot_inv: float32 [4, 4, 64, 256], P('boxx', None, 'boxyz'), may hold values from 0.02 to 0.2
- face_order: int32 [4, 4, 64, 256], P('boxx', None, 'boxyz'), may hold values from 0 to 255, each once within a row
- skel_count: int32 [4, 4, 64], P('boxx', None, 'boxyz'), may hold values from 64 to 128, as said below
- child_pos: int32 [4, 4, 64, 128], P('boxx', None, 'boxyz'), may hold values from 0 to 383, as said below
- owner: int32 [4, 2, 32], P('boxx', None, 'boxyz'), may hold values from 0 to 7, as said below
Outputs:
- parent_blocks: bfloat16 [4, 64, 1, 192, 384], P('boxx', 'boxyz')
The draws below stay inside these ranges and needn't reach their ends.
Inputs may be any that keep to these rules, and one draw needn't show every extreme that they name: `skel_count`: counts per box; some box has exactly 128 and some exactly 64. `child_pos`: the 128 positions of one box are distinct. Entries at first indices 2i and 2i + 1 are equal. The 8 entries of one device are distinct, and owner 8 - 1 is among them on every device.
All inputs are finite; a program needn't handle non-finite values.
Results may differ from the reference program's by a relative error of at most 0.0055.
Values may be sent and summed in bfloat16 or wider, within the bound.
A program may use at most 128 MiB of HBM per device.

```python
import math
import jax
import jax.numpy as jnp
from jax import lax

F = 256
SMAX = 128
PF = 384
BY = 4
BZD = 8
CAP = 1
NXB = 4
NZB = 64
HALF = 8
N_BOXYZ = 8


def draw_skel_count(key, part):
    first, second, third = jax.random.split(key, 3)
    flat_count = NXB * BY * NZB
    values = jax.random.randint(first, (flat_count,), SMAX // 2, SMAX + 1)
    chosen = jax.random.randint(second, (), 0, flat_count)
    lowest = (chosen + 1 + jax.random.randint(third, (), 0, flat_count - 1)) % flat_count
    positions = jnp.arange(flat_count)
    values = jnp.where(positions == chosen, SMAX, values)
    values = jnp.where(positions == lowest, SMAX // 2, values)
    return values.reshape(NXB, BY, NZB).astype(jnp.int32)


def draw_child_pos(key, part):
    flat_count = NXB * BY * NZB
    keys = jax.random.split(key, flat_count)
    rows = jax.vmap(lambda single: jax.random.permutation(single, PF)[:SMAX])(keys)
    return rows.reshape(NXB, BY, NZB, SMAX).astype(jnp.int32)


def draw_owner(key, part):
    owners_count = NZB // BZD
    group_count = BY // 2 * (BZD // 2)
    pair_count = NXB // 2
    block_count = pair_count * owners_count
    keys = jax.random.split(key, block_count)

    def one_block(single):
        first, second = jax.random.split(single, 2)
        others = jax.random.permutation(second, owners_count - 1)[:group_count - 1].astype(jnp.int32)
        values = jnp.concatenate([jnp.full((1,), owners_count - 1, jnp.int32), others])
        return jax.random.permutation(first, values)
    blocks = jax.vmap(one_block)(keys)
    blocks = blocks.reshape(pair_count, owners_count, BY // 2, BZD // 2).transpose(0, 2, 1, 3).reshape(pair_count, BY // 2, NZB // 2)
    return jnp.repeat(blocks, 2, axis=0).astype(jnp.int32)


def block_scale(stream_key, dims, pieces, least, high):
    loudness, own = 1.0, jax.random.fold_in(stream_key, 6)
    for position, blocks in pieces:
        draws = jnp.exp(jax.random.uniform(jax.random.fold_in(own, position), (blocks,), jnp.float32, least / len(pieces), high / len(pieces)))
        loudness = loudness * jnp.repeat(draws, dims[position] // blocks).reshape([-1 if axis == position else 1 for axis in range(len(dims))])
    return loudness


def scatter_about(rng, shape, spread, most, cuts=(), held_as=jnp.bfloat16):
    array = jax.random.normal(rng, shape, jnp.float32) * spread
    if len(cuts) > 0:
        array = block_scale(rng, shape, cuts, -0.22, 0.18) * array
    return jnp.clip(array, min=-most, max=most).astype(held_as)


def setup_inputs(seed: int = 0) -> dict:
    arg_keys = jax.random.split(jax.random.key(seed), 11)
    face_block = scatter_about(arg_keys[0], (NXB, BY, NZB, F, F), F ** -0.5, 0.375, ((0, 4), (2, 8)))
    couple_minus = scatter_about(arg_keys[1], (NXB, BY, NZB, F, F), F ** -0.5, 0.375, ((0, 4), (2, 8)))
    couple_plus = scatter_about(arg_keys[2], (NXB, BY, NZB, F, F), F ** -0.5, 0.375, ((0, 4), (2, 8)))
    couple_up = scatter_about(arg_keys[3], (NXB, BY, NZB, F, F), F ** -0.5, 0.375, ((0, 4), (2, 8)))
    interp = scatter_about(arg_keys[4], (NXB, BY, NZB, F, SMAX), SMAX ** -0.5, 0.5, ((0, 4), (2, 8)))
    pivot_inv = jnp.clip(jnp.exp(math.log(0.2) - 2.3025851 * jax.random.uniform(arg_keys[5], (NXB, BY, NZB, F), jnp.float32) ** block_scale(arg_keys[5], (NXB, BY, NZB, F), ((0, 4), (2, 8)), -0.2, 0.2)), 0.02, 0.2)
    face_order = jax.vmap(lambda own: jax.random.permutation(own, F))(jax.random.split(arg_keys[6], NXB * BY * NZB)).reshape((NXB, BY, NZB, F)).astype(jnp.int32)
    skel_count = draw_skel_count(jax.random.fold_in(arg_keys[10], 71), 0)
    child_pos = draw_child_pos(jax.random.fold_in(arg_keys[10], 71), 0)
    owner = draw_owner(jax.random.fold_in(arg_keys[10], 71), 0)
    return {"face_block": face_block, "couple_minus": couple_minus, "couple_plus": couple_plus, "couple_up": couple_up, "interp": interp, "pivot_inv": pivot_inv, "face_order": face_order, "skel_count": skel_count, "child_pos": child_pos, "owner": owner}


def make_basis(face_list, skel_total, interp_rows):
    row_index = jnp.arange(F, dtype=jnp.int32)[:, None]
    col_index = jnp.arange(SMAX, dtype=jnp.int32)[None, :]
    live_cols = col_index < skel_total
    identity = (row_index == col_index).astype(jnp.float32)
    interp_part = jnp.where(row_index >= skel_total, interp_rows.astype(jnp.float32), jnp.float32(0.0))
    framed = jnp.where(live_cols, identity + interp_part, jnp.float32(0.0))
    inverse = jnp.zeros((F,), jnp.int32).at[face_list.astype(jnp.int32)].set(jnp.arange(F, dtype=jnp.int32))
    box_basis = jnp.take(framed, inverse, axis=0).astype(jnp.bfloat16)
    redundant = (inverse >= skel_total).astype(jnp.float32)
    return box_basis, redundant


def as_float(value):
    return value.astype(jnp.float32)


def reference(face_block, couple_minus, couple_plus, couple_up, interp, pivot_inv, face_order, skel_count, child_pos, owner):
    flat_count = NXB * BY * NZB
    bases, redundant = jax.vmap(make_basis)(face_order.reshape(flat_count, F), skel_count.reshape(flat_count), interp.reshape(flat_count, F, SMAX))
    bases = bases.reshape(NXB, BY, NZB, F, SMAX)
    redundant = redundant.reshape(NXB, BY, NZB, F)
    zero_x = jnp.zeros_like(bases[:1])
    lower_x = jnp.concatenate([zero_x, bases[:-1]], axis=0)
    upper_x = jnp.concatenate([bases[1:], zero_x], axis=0)
    zero_z = jnp.zeros_like(bases[:, :, :1])
    upper_z = jnp.concatenate([bases[:, :, 1:], zero_z], axis=2)

    def plane_skel(items):
        box_block, minus_k, plus_k, up_k, own_basis, lower_rows, higher_rows, above_rows, mask_rows, pivots = items
        own_proj = jnp.einsum('yzif,yzfk->yzik', as_float(box_block), as_float(own_basis)).astype(jnp.bfloat16)
        cross_terms = jnp.einsum('yzif,yzfk->yzik', as_float(minus_k), as_float(lower_rows))
        cross_terms = cross_terms + jnp.einsum('yzif,yzfk->yzik', as_float(plus_k), as_float(higher_rows))
        cross_terms = cross_terms + jnp.einsum('yzif,yzfk->yzik', as_float(up_k), as_float(above_rows))
        coupling = mask_rows[..., None] * (as_float(own_proj) + cross_terms)
        scaled = (coupling * pivots[..., None]).astype(jnp.bfloat16)
        skeleton = jnp.einsum('yzik,yzil->yzkl', as_float(own_basis), as_float(own_proj))
        skeleton = skeleton - jnp.einsum('yzik,yzil->yzkl', as_float(coupling.astype(jnp.bfloat16)), as_float(scaled))
        return skeleton.astype(jnp.bfloat16)

    skeletons = lax.map(plane_skel, (face_block, couple_minus, couple_plus, couple_up, bases, lower_x, upper_x, upper_z, redundant, pivot_inv))
    grouped = skeletons.reshape(NXB, BY // 2, 2, NZB // 2, 2, SMAX, SMAX).transpose(0, 1, 3, 2, 4, 5, 6).reshape(NXB, BY // 2, NZB // 2, 4, SMAX, SMAX)
    places = child_pos.reshape(NXB, BY // 2, 2, NZB // 2, 2, SMAX).transpose(0, 1, 3, 2, 4, 5).reshape(NXB, BY // 2, NZB // 2, 4, SMAX)

    def extend(child_skel, child_places):
        extended = jnp.zeros((PF, PF), jnp.float32)
        return extended.at[child_places[:, :, None], child_places[:, None, :]].add(as_float(child_skel))

    def plane_extend(items):
        child_skel, child_places = items
        return jax.vmap(jax.vmap(extend))(child_skel, child_places).astype(jnp.bfloat16)

    half_blocks = lax.map(plane_extend, (grouped, places))
    parent = (as_float(half_blocks[0::2]) + as_float(half_blocks[1::2])).astype(jnp.bfloat16)
    parent = parent.reshape(NXB // 2, BY // 2, N_BOXYZ, BZD // 2, PF, PF).transpose(0, 2, 1, 3, 4, 5).reshape(NXB // 2, N_BOXYZ, HALF, PF, PF)
    owners = owner[0::2].reshape(NXB // 2, BY // 2, N_BOXYZ, BZD // 2).transpose(0, 2, 1, 3).reshape(NXB // 2, N_BOXYZ, HALF)
    earlier = jnp.arange(HALF, dtype=jnp.int32)[:, None] > jnp.arange(HALF, dtype=jnp.int32)[None, :]
    same_owner = owners[..., :, None] == owners[..., None, :]
    slot_index = jnp.sum((same_owner & earlier).astype(jnp.int32), axis=-1).astype(jnp.int32)
    pair_index = jnp.broadcast_to(jnp.arange(NXB // 2, dtype=jnp.int32)[:, None, None], owners.shape)
    sender = jnp.broadcast_to(jnp.arange(N_BOXYZ, dtype=jnp.int32)[None, :, None], owners.shape)
    placed = jnp.zeros((NXB // 2, N_BOXYZ, N_BOXYZ, CAP, PF, PF), jnp.bfloat16)
    placed = placed.at[pair_index, owners, sender, slot_index].set(parent)
    placed = placed.reshape(NXB // 2, N_BOXYZ, N_BOXYZ, CAP, 2, PF // 2, PF).transpose(0, 4, 1, 2, 3, 5, 6)
    return placed.reshape(NXB, N_BOXYZ * N_BOXYZ, CAP, PF // 2, PF)
```

```python
import functools

import jax
import jax.numpy as jnp
from jax import lax
from jax.experimental import pallas as pl
from jax.experimental.pallas import tpu as pltpu
from jax.sharding import PartitionSpec as P

PF = 384
BF = jnp.bfloat16
F32 = jnp.float32
UNROLL = 4


def iota(shape, dim):
    return lax.broadcasted_iota(jnp.int32, shape, dim)


def dot(a, b):
    return jnp.dot(a, b, preferred_element_type=F32)


def dot_t(a, b):
    return lax.dot_general(a, b, (((1,), (1,)), ((), ())), preferred_element_type=F32)


def framed(packed, count):
    n = packed.shape[0]
    row, col = iota((n, n), 0), iota((n, n), 1)
    zero = jnp.zeros((n, n), F32)
    live = row < count
    left = jnp.where(live & (col >= count), packed.astype(F32).T, zero)
    left = jnp.where(live & (row == col), F32(1.0) + left, left)
    right = jnp.where(live, packed.astype(F32), zero)
    return jnp.concatenate([left, right], axis=1).astype(BF)


def one_hot(order, size):
    return jnp.where(order == iota((size, order.shape[1]), 0), F32(1.0), F32(0.0)).astype(BF)


def kernel(nx, nyz, by, bzd, fb, cm, cp, cu, interp, face_order, counts, pivots, pos, owner,
           out,
           fb_v, cm_v, cp_v, cu_v, ip_v, pk, lo, hi, ze, meta, meta_lo, meta_hi, meta_z,
           piv, bas, red, acc, sk1, lift, place, give, got, keep, outb,
           in_sem, ip_sem, up_s, up_r, dn_s, dn_r, z_s, z_r, pt_s, pt_r, o_s, o_r, own_sem):
    boxes, face, smax = interp.shape
    rows = outb.shape[1]
    x = lax.axis_index("boxx")
    me = lax.axis_index("boxyz")
    parity = lax.rem(x, 2)
    partner = x + 1 - 2 * parity
    half = nyz // 2
    groups_z = bzd // 2
    groups = (by // 2) * groups_z

    barrier = pltpu.get_barrier_semaphore()
    for j in range(1, nyz):
        pl.semaphore_signal(barrier, inc=1, device_id={"boxyz": lax.rem(me + j, nyz)})

    @pl.when(x > 0)
    def _():
        pl.semaphore_signal(barrier, inc=1, device_id={"boxx": x - 1})

    @pl.when(x < nx - 1)
    def _():
        pl.semaphore_signal(barrier, inc=1, device_id={"boxx": x + 1})

    def local_in(src, dst, sem, y):
        part = pl.ds(y * bzd, bzd)
        return pltpu.make_async_copy(src.at[part], dst.at[part], sem)

    big = ((fb, fb_v), (cu, cu_v), (cm, cm_v), (cp, cp_v))
    for y in range(by):
        local_in(interp, ip_v, ip_sem.at[y], y).start()

    def up_copy(y):
        if y == by:
            src, dst = meta, meta_lo
        else:
            src, dst = pk.at[pl.ds(y * bzd, bzd)], lo.at[pl.ds(y * bzd, bzd)]
        return pltpu.make_async_remote_copy(
            src, dst, up_s.at[y], up_r.at[y], device_id={"boxx": x + 1})

    def down_copy(y):
        if y == by:
            src, dst = meta, meta_hi
        else:
            src, dst = pk.at[pl.ds(y * bzd, bzd)], hi.at[pl.ds(y * bzd, bzd)]
        return pltpu.make_async_remote_copy(
            src, dst, dn_s.at[y], dn_r.at[y], device_id={"boxx": x - 1})

    def z_copy(y):
        src, dst = (meta, meta_z) if y == by else (pk.at[y * bzd], ze.at[y])
        return pltpu.make_async_remote_copy(
            src, dst, z_s.at[y], z_r.at[y], device_id={"boxyz": me - 1})

    def start_copies(y):
        @pl.when(me > 0)
        def _():
            z_copy(y).start()

        @pl.when(x > 0)
        def _():
            down_copy(y).start()

        @pl.when(x < nx - 1)
        def _():
            up_copy(y).start()

    for b in range(boxes):
        y, z = b // bzd, b % bzd
        meta[b, :, :face] = face_order[y, z:z + 1, :]
        meta[b, :, face:] = jnp.full((1, smax), counts[y, z], jnp.int32)
        piv[b] = pivots[y, z:z + 1, :]

    def pack(b, carry):
        block = ip_v[b]
        count = meta[b][:, face:]
        bottom = block[smax:].astype(F32).T
        pk[b] = jnp.where(
            iota((smax, smax), 0) < count, bottom, block[:smax].astype(F32)).astype(BF)
        return carry

    order = [[k for k in range(4) if min(k + 1, by - 1) == y] for y in range(by)]
    for y in range(by):
        local_in(interp, ip_v, ip_sem.at[y], y).wait()
        lax.fori_loop(y * bzd, (y + 1) * bzd, pack, 0, unroll=UNROLL)
        if y == 0:
            pl.semaphore_wait(
                barrier, nyz - 1 + jnp.minimum(x, 1) + jnp.minimum(nx - 1 - x, 1))
            start_copies(by)
        start_copies(y)
        for k in order[y]:
            src, dst = big[k]
            for part in range(by):
                local_in(src, dst, in_sem.at[k * by + part], part).start()

    @pl.when(x == 0)
    def _():
        meta_lo[...] = jnp.zeros_like(meta_lo)

    @pl.when(x == nx - 1)
    def _():
        meta_hi[...] = jnp.zeros_like(meta_hi)

    @pl.when(me == nyz - 1)
    def _():
        meta_z[...] = jnp.zeros_like(meta_z)

    def own_basis(b, carry):
        info = meta[b]
        count = info[:, face:]
        wide = jnp.concatenate([count, count], axis=1)
        rest = jnp.where(iota((16, face), 1) >= wide, F32(1.0), F32(0.0)).astype(BF)
        frame = jnp.concatenate([framed(pk[b], count), rest], axis=0)
        both = dot_t(frame, one_hot(info[:, :face], face))
        bas[b + lax.div(b, bzd)] = both[:smax].astype(BF)
        red[b] = both[smax:smax + 1]
        return carry

    lax.fori_loop(0, boxes, own_basis, 0, unroll=UNROLL)

    def received(packed, info):
        return dot_t(framed(packed, info[:, face:]), one_hot(info[:, :face], face)).astype(BF)

    @pl.when(me < nyz - 1)
    def _():
        for y in range(by + 1):
            z_copy(y).wait_recv()

    for y in range(by):
        bas[y * (bzd + 1) + bzd] = received(ze[y], meta_z[y * bzd])

    def own_part(b, carry):
        at = b + lax.div(b, bzd)
        basis = bas[at]
        proj = dot_t(basis, fb_v[b]).astype(BF)
        sk1[b] = dot_t(basis, proj)
        acc[b] = proj.astype(F32) + dot_t(bas[at + 1], cu_v[b])
        return carry

    for y in range(by):
        local_in(fb, fb_v, in_sem.at[y], y).wait()
        local_in(cu, cu_v, in_sem.at[by + y], y).wait()
        lax.fori_loop(y * bzd, (y + 1) * bzd, own_part, 0, unroll=UNROLL)

    for k in (2, 3):
        for y in range(by):
            local_in(big[k][0], big[k][1], in_sem.at[k * by + y], y).wait()

    @pl.when(x > 0)
    def _():
        for y in range(by + 1):
            up_copy(y).wait_recv()

    @pl.when(x < nx - 1)
    def _():
        for y in range(by + 1):
            down_copy(y).wait_recv()

    def dest_of(s):
        far = 1 - lax.div(s, half)
        side = lax.div(me, half)
        side = side + far - 2 * side * far
        return side * half + lax.rem(lax.rem(me, half) + s + 1 - far, half)

    def partner_copy(s):
        return pltpu.make_async_remote_copy(
            give.at[s], got.at[s], pt_s.at[s], pt_r.at[s], device_id={"boxx": partner})

    def out_copy(s):
        return pltpu.make_async_remote_copy(
            outb.at[s], out.at[me], o_s.at[s], o_r.at[me], device_id={"boxyz": dest_of(s)})

    def add_partner(s):
        partner_copy(s).wait_recv()
        outb[s] = (keep[s].astype(F32) + got[s].astype(F32)).astype(BF)

    def group(s, carry):
        dest = dest_of(s)
        g, valid = jnp.int32(0), jnp.int32(0)
        for h in range(groups):
            hit = owner[h // groups_z, h % groups_z] == dest
            g, valid = jnp.where(hit, h, g), jnp.where(hit, 1, valid)
        first = lax.div(g, groups_z) * (2 * bzd) + lax.rem(g, groups_z) * 2
        for c in range(4):
            b = first + (c // 2) * bzd + c % 2
            low = received(lo[b], meta_lo[b])
            high = received(hi[b], meta_hi[b])
            total = acc[b] + dot_t(low, cm_v[b]) + dot_t(high, cp_v[b])
            coupling = red[b] * total
            scaled = (coupling * piv[b]).astype(BF)
            skel = (sk1[b] - dot_t(coupling.astype(BF), scaled)).astype(BF)
            spot = one_hot(pos[b], PF)
            place[:, c * smax:(c + 1) * smax] = spot
            lift[:, c * smax:(c + 1) * smax] = dot(spot, skel).astype(BF)
        spots = place[...]

        def rows_at(which):
            start = pl.multiple_of(which * rows, rows)
            value = dot_t(lift[pl.ds(start, rows), :], spots)
            return jnp.where(valid > 0, value, F32(0.0)).astype(BF)

        give[s] = rows_at(1 - parity)
        partner_copy(s).start()
        keep[s] = rows_at(parity)

        @pl.when(s == 0)
        def _():
            add_partner(s)
            out_copy(s).start()

        @pl.when(s > 1)
        def _():
            add_partner(s - 1)
            out_copy(s - 1).start()

        return carry

    lax.fori_loop(0, nyz, group, 0)
    last = nyz - 1
    add_partner(last)
    own = pltpu.make_async_copy(outb.at[last], out.at[me], own_sem)
    own.start()

    @pl.when(me > 0)
    def _():
        for y in range(by + 1):
            z_copy(y).wait_send()

    @pl.when(x > 0)
    def _():
        for y in range(by + 1):
            down_copy(y).wait_send()

    @pl.when(x < nx - 1)
    def _():
        for y in range(by + 1):
            up_copy(y).wait_send()

    for s in range(nyz):
        partner_copy(s).wait_send()
    for s in range(nyz - 1):
        out_copy(s).wait_send()
    own.wait()
    for j in range(1, nyz):
        q = lax.rem(me + j, nyz)
        pltpu.make_async_remote_copy(
            outb.at[0], out.at[q], o_s.at[0], o_r.at[q], device_id={"boxyz": q}).wait_recv()


def shards(nx, nyz, face_block, couple_minus, couple_plus, couple_up, interp, pivot_inv,
           face_order, skel_count, child_pos, owner):
    _, by, bzd, face, smax = interp.shape
    boxes = by * bzd
    rows = PF // 2
    square = (boxes, face, face)
    slim = (boxes, face, smax)
    thin = (boxes, smax, face)
    any_ = pl.BlockSpec(memory_space=pl.ANY)
    vmem = pl.BlockSpec(memory_space=pltpu.VMEM)
    smem = pl.BlockSpec(memory_space=pltpu.SMEM)
    dma = pltpu.SemaphoreType.DMA
    out = pl.pallas_call(
        functools.partial(kernel, nx, nyz, by, bzd),
        name="eliminate",
        out_shape=pltpu.VMEM((nyz, rows, PF), BF),
        in_specs=[any_] * 5 + [vmem, smem, vmem, vmem, smem],
        out_specs=vmem,
        scratch_shapes=[pltpu.VMEM(square, BF)] * 4
        + [pltpu.VMEM(slim, BF)]
        + [pltpu.VMEM((boxes, smax, smax), BF)] * 3
        + [pltpu.VMEM((by, smax, smax), BF)]
        + [pltpu.VMEM((boxes, 1, face + smax), jnp.int32)] * 4
        + [pltpu.VMEM((boxes, 1, face), F32),
           pltpu.VMEM((by * (bzd + 1), smax, face), BF),
           pltpu.VMEM((boxes, 1, face), F32),
           pltpu.VMEM(thin, F32),
           pltpu.VMEM((boxes, smax, smax), F32)]
        + [pltpu.VMEM((PF, 4 * smax), BF)] * 2
        + [pltpu.VMEM((nyz, rows, PF), BF)] * 4
        + [dma((4 * by,)), dma((by,))]
        + [dma((by + 1,))] * 6
        + [dma((nyz,))] * 4
        + [dma],
        compiler_params=pltpu.CompilerParams(
            collective_id=0, has_side_effects=True, vmem_limit_bytes=58 << 20),
    )(face_block.reshape(square), couple_minus.reshape(square), couple_plus.reshape(square),
      couple_up.reshape(square), interp.reshape(slim),
      face_order.reshape(by, bzd, face), skel_count.reshape(by, bzd),
      pivot_inv.reshape(by, bzd, face), child_pos.reshape(boxes, 1, smax),
      owner.reshape(by // 2, bzd // 2))
    return out.reshape(1, nyz, 1, rows, PF)


def solution(mesh):
    return jax.shard_map(
        functools.partial(shards, mesh.shape["boxx"], mesh.shape["boxyz"]),
        mesh=mesh,
        in_specs=(P("boxx", None, "boxyz", None, None),) * 5
        + (P("boxx", None, "boxyz", None),) * 2
        + (P("boxx", None, "boxyz"), P("boxx", None, "boxyz", None), P("boxx", None, "boxyz")),
        out_specs=P("boxx", "boxyz", None, None, None),
        check_vma=False,
    )
```

```python
import functools

import jax
import jax.numpy as jnp
from jax import lax
from jax.experimental import pallas as pl
from jax.experimental.pallas import tpu as pltpu
from jax.sharding import PartitionSpec as P

PF = 384
BF = jnp.bfloat16
F32 = jnp.float32
I32 = jnp.int32


def iota(shape, dim):
    return lax.broadcasted_iota(I32, shape, dim)


def dot(a, b):
    return jnp.dot(a, b, preferred_element_type=F32)


def dot_t(a, b):
    return lax.dot_general(a, b, (((1,), (1,)), ((), ())), preferred_element_type=F32)


def framed(packed, count):
    n = packed.shape[0]
    row, col = iota((n, n), 0), iota((n, n), 1)
    zero = jnp.zeros((n, n), F32)
    live = row < count
    left = jnp.where(live & (col >= count), packed.astype(F32).T, zero)
    left = jnp.where(live & (row == col), F32(1.0) + left, left)
    right = jnp.where(live, packed.astype(F32), zero)
    return jnp.concatenate([left, right], axis=1).astype(BF)


def one_hot(order, size):
    return jnp.where(order == iota((size, order.shape[1]), 0), F32(1.0), F32(0.0)).astype(BF)


def steps_between(n, moves):
    worst = 0
    for start in range(n):
        seen, edge, far = {start}, {start}, 0
        while len(seen) < n:
            edge = {p + m for p in edge for m in moves if 0 <= p + m < n} - seen
            seen |= edge
            far += 1
        worst = max(worst, far)
    return worst


def near_moves(nyz):
    wide = 1 << ((nyz.bit_length() - 1) // 2)
    return tuple(sorted({1, -1, wide, -wide}))


def kernel(nx, nyz, by, bzd, fb, cm, cp, cu, interp, face_order, counts, pivots, pos, owner,
           out,
           fb_v, cu_v, co_v, ip_v, pk, stf, far, ze, meta, meta_f, meta_z, piv, red, bas,
           stp, par, acc, sk1, skl, rcv, fwd, posb, posr, half, owner_f, ord_o, ord_f,
           in_sem, ip_sem, z_s, z_r, mz_s, mz_r, mf_s, mf_r, of_s, of_r, pp_s, pp_r,
           p_s, p_r, f_s, f_r, o_s, o_r, po_s, po_r, w_s, w_r, relay):
    face, smax = interp.shape[2:]
    rows = out.shape[1]
    x = lax.axis_index("boxx")
    me = lax.axis_index("boxyz")
    parity = lax.rem(x, 2)
    partner = x + 1 - 2 * parity
    other = x - 1 + 2 * parity
    has_far = (other >= 0) & (other < nx)
    middle = nyz // 2
    last = nyz - 1
    groups_z = bzd // 2
    groups = (by // 2) * groups_z
    moves = near_moves(nyz)

    barrier = pltpu.get_barrier_semaphore()
    pl.semaphore_signal(barrier, inc=1, device_id={"boxx": partner})

    @pl.when(has_far)
    def _():
        pl.semaphore_signal(barrier, inc=1, device_id={"boxx": other})

    def there(m):
        return (me + m >= 0) & (me + m < nyz)

    def greet(sem):
        for m in moves:
            @pl.when(there(m))
            def _(m=m):
                pl.semaphore_signal(sem, inc=1, device_id={"boxyz": me + m})

    near = jnp.int32(0)
    for m in moves:
        near = near + jnp.where(there(m), 1, 0)
    greet(barrier)

    for y in range(by):
        pltpu.make_async_copy(interp.at[y], ip_v.at[y], ip_sem.at[y]).start()
    big = ((fb, fb_v), (cu, cu_v), (cm, co_v.at[parity]), (cp, co_v.at[1 - parity]))

    def load(k, y):
        return pltpu.make_async_copy(big[k][0].at[y], big[k][1].at[y], in_sem.at[k * by + y])

    def dest_of(s):
        far_side = 1 - lax.div(s, middle)
        side = lax.div(me, middle)
        side = side + far_side - 2 * side * far_side
        return side * middle + lax.rem(lax.rem(me, middle) + s + 1 - far_side, middle)

    def source_of(s):
        far_side = 1 - lax.div(s, middle)
        side = lax.div(me, middle)
        side = side + far_side - 2 * side * far_side
        return side * middle + lax.rem(
            lax.rem(me, middle) + 2 * middle - s - 1 + far_side, middle)

    def search(table, s):
        dest = dest_of(s)
        g, valid = jnp.int32(0), jnp.int32(0)
        for h in range(groups):
            hit = table[h // groups_z, h % groups_z] == dest
            g, valid = jnp.where(hit, h, g), jnp.where(hit, 1, valid)
        return g, valid

    def child(g, c):
        return 2 * lax.div(g, groups_z) + c // 2, 2 * lax.rem(g, groups_z) + c % 2

    for y in range(by):
        for z in range(bzd):
            meta[y, z, :, :face] = face_order[y, z:z + 1, :]
            meta[y, z, :, face:] = jnp.full((1, smax), counts[y, z], I32)
            piv[y, z] = pivots[y, z:z + 1, :]

    def arrange(s, carry):
        g, valid = search(owner, s)
        ord_o[s] = g
        for c in range(4):
            y, z = child(g, c)
            posb[0, s, c] = jnp.where(valid > 0, pos[y, z], -1)
        return carry

    lax.fori_loop(0, nyz, arrange, 0)

    def pack(y):
        for z in range(bzd):
            block = ip_v[y, z]
            count = meta[y, z][:, face:]
            bottom = block[smax:].astype(F32).T
            pk[y, z] = jnp.where(
                iota((smax, smax), 0) < count, bottom, block[:smax].astype(F32)).astype(BF)

    order = [[k for k in range(4) if min(k + 1, by - 1) == y] for y in range(by)]
    for y in range(by):
        pltpu.make_async_copy(interp.at[y], ip_v.at[y], ip_sem.at[y]).wait()
        pack(y)
        for k in order[y]:
            for part in range(by):
                load(k, part).start()

    def z_copy():
        return pltpu.make_async_remote_copy(
            pk.at[:, 0], ze, z_s, z_r, device_id={"boxyz": me - 1})

    def mz_copy():
        return pltpu.make_async_remote_copy(
            meta.at[:, 0], meta_z, mz_s, mz_r, device_id={"boxyz": me - 1})

    def mf_copy():
        return pltpu.make_async_remote_copy(
            meta, meta_f, mf_s, mf_r, device_id={"boxx": other})

    def of_copy():
        return pltpu.make_async_remote_copy(
            owner, owner_f, of_s, of_r, device_id={"boxx": other})

    def pp_copy():
        return pltpu.make_async_remote_copy(
            posb.at[0], posb.at[1], pp_s, pp_r, device_id={"boxx": partner})

    def par_copy(s):
        return pltpu.make_async_remote_copy(
            stp.at[s], par.at[s], p_s.at[s], p_r.at[s], device_id={"boxx": partner})

    def far_copy(s):
        return pltpu.make_async_remote_copy(
            stf.at[s], far.at[s], f_s.at[s], f_r.at[s], device_id={"boxx": other})

    def out_copy(s):
        return pltpu.make_async_remote_copy(
            skl.at[s], rcv.at[s], o_s.at[s], o_r.at[s], device_id={"boxyz": dest_of(s)})

    def pos_copy(s):
        return pltpu.make_async_remote_copy(
            posb.at[:, s], posr.at[:, s], po_s.at[s], po_r.at[s],
            device_id={"boxyz": dest_of(s)})

    def fwd_copy(s):
        return pltpu.make_async_remote_copy(
            rcv.at[s], fwd.at[s], w_s.at[s], w_r.at[s], device_id={"boxx": partner})

    def own_basis(y, carry):
        for z in range(bzd):
            info = meta[y, z]
            count = info[:, face:]
            wide = jnp.concatenate([count, count], axis=1)
            rest = jnp.where(iota((16, face), 1) >= wide, F32(1.0), F32(0.0)).astype(BF)
            frame = jnp.concatenate([framed(pk[y, z], count), rest], axis=0)
            both = dot_t(frame, one_hot(info[:, :face], face))
            bas[y, z] = both[:smax].astype(BF)
            red[y, z] = both[smax:smax + 1]
        return carry

    early = by // 2
    lax.fori_loop(0, early, own_basis, 0)

    pl.semaphore_wait(barrier, near + 1 + jnp.where(has_far, 1, 0))
    rounds = steps_between(nyz, moves) - 1
    greet(relay.at[0])

    @pl.when(me > 0)
    def _():
        mz_copy().start()
        z_copy().start()

    @pl.when(has_far)
    def _():
        of_copy().start()
        mf_copy().start()

    pp_copy().start()
    lax.fori_loop(early, by, own_basis, 0)

    def stage_partner(s, carry):
        g = ord_o[s]
        for c in range(4):
            y, z = child(g, c)
            stp[s, c] = bas[y, z]
        par_copy(s).start()
        return carry

    lax.fori_loop(0, 1, stage_partner, 0)

    @pl.when(has_far)
    def _():
        of_copy().wait_recv()

        def stage_far(s, carry):
            g, _ = search(owner_f, s)
            for c in range(4):
                y, z = child(g, c)
                stf[s, c] = pk[y, z]
            far_copy(s).start()
            return carry

        lax.fori_loop(0, nyz, stage_far, 0)

    for k in range(1, rounds):
        pl.semaphore_wait(relay.at[k - 1], near)
        greet(relay.at[k])

    lax.fori_loop(1, nyz, stage_partner, 0)

    def received(packed, info):
        return dot_t(framed(packed, info[:, face:]), one_hot(info[:, :face], face)).astype(BF)

    @pl.when(me == last)
    def _():
        meta_z[...] = jnp.zeros_like(meta_z)

    @pl.when(me < last)
    def _():
        mz_copy().wait_recv()
        z_copy().wait_recv()

    for y in range(by):
        bas[y, bzd] = received(ze[y], meta_z[y])

    @pl.when(has_far)
    def _():
        mf_copy().wait_recv()

    for k in range(4):
        for y in range(by):
            load(k, y).wait()

    def first_half(s):
        g = ord_o[s]
        slot = lax.rem(s, 2)
        for c in range(4):
            y, z = child(g, c)
            basis = bas[y, z]
            proj = dot_t(basis, fb_v[y, z]).astype(BF)
            sk1[slot, c] = dot_t(basis, proj)
            acc[slot, c] = (proj.astype(F32) + dot_t(bas[y, z + 1], cu_v[y, z])
                            + dot_t(par[s, c], co_v[1, y, z]))

    def second_half(s, with_far):
        g = ord_o[s]
        slot = lax.rem(s, 2)
        for c in range(4):
            y, z = child(g, c)
            total = acc[slot, c]
            if with_far:
                total = total + dot_t(received(far[s, c], meta_f[y, z]), co_v[0, y, z])
            coupling = red[y, z] * total
            scaled = (coupling * piv[y, z]).astype(BF)
            skl[s, c] = (sk1[slot, c] - dot_t(coupling.astype(BF), scaled)).astype(BF)

    def send_pos(s, carry):
        pos_copy(s).start()
        return carry

    def all_groups(with_far):
        def arrive(s):
            if with_far:
                far_copy(s).wait_recv()

        par_copy(0).wait_recv()
        first_half(jnp.int32(0))
        arrive(0)
        second_half(jnp.int32(0), with_far)
        for k in range(rounds - 1, rounds):
            pl.semaphore_wait(relay.at[k], near)
        out_copy(0).start()
        pp_copy().wait_recv()
        lax.fori_loop(0, last, send_pos, 0)
        par_copy(1).wait_recv()
        first_half(jnp.int32(1))

        def step(s, carry):
            par_copy(s + 1).wait_recv()
            arrive(s)
            second_half(s, with_far)
            first_half(s + 1)
            out_copy(s).start()
            return carry

        lax.fori_loop(1, last, step, 0)
        arrive(last)
        second_half(jnp.int32(last), with_far)

    @pl.when(has_far)
    def _():
        all_groups(True)

    @pl.when(jnp.logical_not(has_far))
    def _():
        all_groups(False)

    rcv[last] = skl[last]
    posr[:, last] = posb[:, last]

    def expand(blocks, places):
        spots = [one_hot(places[c], PF) for c in range(4)]
        lifts = [dot(one_hot(places[c] - parity * rows, rows), blocks[c]).astype(BF)
                 for c in range(4)]
        return dot_t(jnp.concatenate(lifts, axis=1), jnp.concatenate(spots, axis=1)).astype(BF)

    def slot_at(j):
        odd = lax.rem(j, 2)
        return jnp.where(odd == 1, lax.div(j, 2), middle + lax.div(j, 2) - 1)

    def arrived(s):
        out_copy(s).wait_recv()
        pos_copy(s).wait_recv()
        fwd_copy(s).start()

    def own_side(s):
        half[s] = expand([rcv[s, c] for c in range(4)], [posr[0, s, c] for c in range(4)])

    def partner_side(s):
        value = expand([fwd[s, c] for c in range(4)], [posr[1, s, c] for c in range(4)])
        out[source_of(s)] = (half[s].astype(F32) + value.astype(F32)).astype(BF)

    fwd_copy(last).start()
    own_side(last)
    arrived(slot_at(jnp.int32(1)))
    own_side(slot_at(jnp.int32(1)))
    fwd_copy(last).wait_recv()
    partner_side(last)

    def merge(j, carry):
        now, before = slot_at(j), slot_at(j - 1)
        arrived(now)
        fwd_copy(before).wait_recv()
        own_side(now)
        partner_side(before)
        return carry

    lax.fori_loop(2, nyz, merge, 0)
    final = slot_at(jnp.int32(last))
    fwd_copy(final).wait_recv()
    partner_side(final)

    @pl.when(me > 0)
    def _():
        z_copy().wait_send()
        mz_copy().wait_send()

    @pl.when(has_far)
    def _():
        of_copy().wait_send()
        mf_copy().wait_send()
        for s in range(nyz):
            far_copy(s).wait_send()

    pp_copy().wait_send()
    for s in range(nyz):
        par_copy(s).wait_send()
        fwd_copy(s).wait_send()
    for s in range(last):
        out_copy(s).wait_send()
        pos_copy(s).wait_send()


def shards(nx, nyz, face_block, couple_minus, couple_plus, couple_up, interp, pivot_inv,
           face_order, skel_count, child_pos, owner):
    _, by, bzd, face, smax = interp.shape
    rows = PF // 2
    any_ = pl.BlockSpec(memory_space=pl.ANY)
    vmem = pl.BlockSpec(memory_space=pltpu.VMEM)
    smem = pl.BlockSpec(memory_space=pltpu.SMEM)
    dma = pltpu.SemaphoreType.DMA
    small = (smax, smax)
    rounds = steps_between(nyz, near_moves(nyz)) - 1
    out = pl.pallas_call(
        functools.partial(kernel, nx, nyz, by, bzd),
        name="eliminate",
        out_shape=pltpu.VMEM((nyz, rows, PF), BF),
        in_specs=[any_] * 5 + [vmem, smem, vmem, vmem, smem],
        out_specs=vmem,
        scratch_shapes=[pltpu.VMEM((by, bzd, face, face), BF)] * 2
        + [pltpu.VMEM((2, by, bzd, face, face), BF)]
        + [pltpu.VMEM((by, bzd, face, smax), BF)]
        + [pltpu.VMEM((by, bzd) + small, BF)]
        + [pltpu.VMEM((nyz, 4) + small, BF)] * 2
        + [pltpu.VMEM((by,) + small, BF)]
        + [pltpu.VMEM((by, bzd, 1, face + smax), I32)] * 2
        + [pltpu.VMEM((by, 1, face + smax), I32)]
        + [pltpu.VMEM((by, bzd, 1, face), F32)] * 2
        + [pltpu.VMEM((by, bzd + 1, smax, face), BF)]
        + [pltpu.VMEM((nyz, 4, smax, face), BF)] * 2
        + [pltpu.VMEM((2, 4, smax, face), F32)]
        + [pltpu.VMEM((2, 4) + small, F32)]
        + [pltpu.VMEM((nyz, 4) + small, BF)] * 3
        + [pltpu.VMEM((2, nyz, 4, 1, smax), I32)] * 2
        + [pltpu.VMEM((nyz, rows, PF), BF)]
        + [pltpu.SMEM((by // 2, bzd // 2), I32)]
        + [pltpu.SMEM((nyz,), I32)] * 2
        + [dma((4 * by,)), dma((by,))]
        + [dma] * 10
        + [dma((nyz,))] * 10
        + [pltpu.SemaphoreType.REGULAR((rounds,))],
        compiler_params=pltpu.CompilerParams(
            collective_id=0, has_side_effects=True, vmem_limit_bytes=58 << 20),
    )(face_block[0], couple_minus[0], couple_plus[0], couple_up[0], interp[0],
      face_order[0], skel_count[0], pivot_inv[0],
      child_pos.reshape(by, bzd, 1, smax), owner[0].reshape(by // 2, bzd // 2))
    return out.reshape(1, nyz, 1, rows, PF)


def solution(mesh):
    return jax.shard_map(
        functools.partial(shards, mesh.shape["boxx"], mesh.shape["boxyz"]),
        mesh=mesh,
        in_specs=(P("boxx", None, "boxyz", None, None),) * 5
        + (P("boxx", None, "boxyz", None),) * 2
        + (P("boxx", None, "boxyz"), P("boxx", None, "boxyz", None), P("boxx", None, "boxyz")),
        out_specs=P("boxx", "boxyz", None, None, None),
        check_vma=False,
    )
```

```python
import functools

import jax
import jax.numpy as jnp
from jax import lax
from jax.experimental import pallas as pl
from jax.experimental.pallas import tpu as pltpu
from jax.sharding import PartitionSpec as P

PF = 384
BF = jnp.bfloat16
F32 = jnp.float32
I32 = jnp.int32


def iota(shape, dim):
    return lax.broadcasted_iota(I32, shape, dim)


def dot(a, b):
    return jnp.dot(a, b, preferred_element_type=F32)


def dot_t(a, b):
    return lax.dot_general(a, b, (((1,), (1,)), ((), ())), preferred_element_type=F32)


def framed(packed, count):
    n = packed.shape[0]
    row, col = iota((n, n), 0), iota((n, n), 1)
    zero = jnp.zeros((n, n), F32)
    live = row < count
    left = jnp.where(live & (col >= count), packed.astype(F32).T, zero)
    left = jnp.where(live & (row == col), F32(1.0) + left, left)
    right = jnp.where(live, packed.astype(F32), zero)
    return jnp.concatenate([left, right], axis=1).astype(BF)


def one_hot(order, size):
    return jnp.where(order == iota((size, order.shape[1]), 0), F32(1.0), F32(0.0)).astype(BF)


def steps_between(n, moves):
    worst = 0
    for start in range(n):
        seen, edge, far = {start}, {start}, 0
        while len(seen) < n:
            edge = {p + m for p in edge for m in moves if 0 <= p + m < n} - seen
            seen |= edge
            far += 1
        worst = max(worst, far)
    return worst


def near_moves(nyz):
    wide = 1 << ((nyz.bit_length() - 1) // 2)
    return tuple(sorted({1, -1, wide, -wide}))


def kernel(nx, nyz, by, bzd, fb, cm, cp, cu, interp, face_order, counts, pivots, pos, owner,
           out,
           fb_v, cu_v, co_v, ip_v, fo_v, pv_v, ps_v, pk, stf, far, ze, meta, meta_f, meta_z, piv, red, bas,
           stp, par, acc, sk1, skl, rcv, fwd, posb, posr, half, fbas, owner_f, ord_o, ord_f,
           in_sem, ip_sem, small_sem, z_s, z_r, mz_s, mz_r, mf_s, mf_r, of_s, of_r, pp_s, pp_r,
           p_s, p_r, f_s, f_r, o_s, o_r, po_s, po_r, w_s, w_r, relay):
    face, smax = interp.shape[2:]
    rows = out.shape[1]
    x = lax.axis_index("boxx")
    me = lax.axis_index("boxyz")
    parity = lax.rem(x, 2)
    partner = x + 1 - 2 * parity
    other = x - 1 + 2 * parity
    has_far = (other >= 0) & (other < nx)
    middle = nyz // 2
    last = nyz - 1
    groups_z = bzd // 2
    groups = (by // 2) * groups_z
    moves = near_moves(nyz)

    def small(k):
        src, dst = ((face_order, fo_v), (pivots, pv_v), (pos, ps_v))[k]
        return pltpu.make_async_copy(src, dst, small_sem.at[k])

    def interp_copy(y):
        return pltpu.make_async_copy(interp.at[y], ip_v.at[y], ip_sem.at[y])

    big = ((fb, fb_v), (cu, cu_v), (cm, co_v.at[parity]), (cp, co_v.at[1 - parity]))

    def load(k, y):
        return pltpu.make_async_copy(big[k][0].at[y], big[k][1].at[y], in_sem.at[k * by + y])

    small(0).start()
    for y in range(by):
        interp_copy(y).start()
    for k in (1, 2):
        small(k).start()

    barrier = pltpu.get_barrier_semaphore()
    pl.semaphore_signal(barrier, inc=1, device_id={"boxx": partner})

    @pl.when(has_far)
    def _():
        pl.semaphore_signal(barrier, inc=1, device_id={"boxx": other})

    def there(m):
        return (me + m >= 0) & (me + m < nyz)

    def greet(sem):
        for m in moves:
            @pl.when(there(m))
            def _(m=m):
                pl.semaphore_signal(sem, inc=1, device_id={"boxyz": me + m})

    near = jnp.int32(0)
    for m in moves:
        near = near + jnp.where(there(m), 1, 0)
    greet(barrier)

    def dest_of(s):
        mask = jnp.where(lax.rem(s, 2) == 0, middle, 0) + lax.rem(lax.div(s + 1, 2), middle)
        dest, bit = jnp.int32(0), 1
        while bit < nyz:
            mine, flip = lax.rem(lax.div(me, bit), 2), lax.rem(lax.div(mask, bit), 2)
            dest = dest + bit * (mine + flip - 2 * mine * flip)
            bit *= 2
        return dest

    def search(table, s):
        dest = dest_of(s)
        g, valid = jnp.int32(0), jnp.int32(0)
        for h in range(groups):
            hit = table[h // groups_z, h % groups_z] == dest
            g, valid = jnp.where(hit, h, g), jnp.where(hit, 1, valid)
        return g, valid

    def child(g, c):
        return 2 * lax.div(g, groups_z) + c // 2, 2 * lax.rem(g, groups_z) + c % 2

    small(0).wait()
    for y in range(by):
        for z in range(bzd):
            meta[y, z, :, :face] = fo_v[y, z:z + 1, :]
            meta[y, z, :, face:] = jnp.full((1, smax), counts[y, z], I32)

    def pack(y):
        for z in range(bzd):
            block = ip_v[y, z]
            count = meta[y, z][:, face:]
            bottom = block[smax:].astype(F32).T
            pk[y, z] = jnp.where(
                iota((smax, smax), 0) < count, bottom, block[:smax].astype(F32)).astype(BF)

    order = [[k for k in range(4) if min(k, by - 1) == y] for y in range(by)]
    for y in range(by):
        interp_copy(y).wait()
        for k in order[y]:
            for part in range(by):
                load(k, part).start()
        pack(y)

    def arrange(s, carry):
        g, valid = search(owner, s)
        ord_o[s] = g
        for c in range(4):
            y, z = child(g, c)
            posb[0, s, c] = jnp.where(valid > 0, ps_v[y, z], -1)
        return carry

    def z_copy():
        return pltpu.make_async_remote_copy(
            pk.at[:, 0], ze, z_s, z_r, device_id={"boxyz": me - 1})

    def mz_copy():
        return pltpu.make_async_remote_copy(
            meta.at[:, 0], meta_z, mz_s, mz_r, device_id={"boxyz": me - 1})

    def mf_copy():
        return pltpu.make_async_remote_copy(
            meta, meta_f, mf_s, mf_r, device_id={"boxx": other})

    def of_copy():
        return pltpu.make_async_remote_copy(
            owner, owner_f, of_s, of_r, device_id={"boxx": other})

    def pp_copy():
        return pltpu.make_async_remote_copy(
            posb.at[0], posb.at[1], pp_s, pp_r, device_id={"boxx": partner})

    def par_copy(s):
        return pltpu.make_async_remote_copy(
            stp.at[s], par.at[s], p_s.at[s], p_r.at[s], device_id={"boxx": partner})

    def far_copy(s):
        return pltpu.make_async_remote_copy(
            stf.at[s], far.at[s], f_s.at[s], f_r.at[s], device_id={"boxx": other})

    def out_copy(s):
        return pltpu.make_async_remote_copy(
            skl.at[s], rcv.at[s], o_s.at[s], o_r.at[s], device_id={"boxyz": dest_of(s)})

    def pos_copy(s):
        return pltpu.make_async_remote_copy(
            posb.at[:, s], posr.at[:, s], po_s.at[s], po_r.at[s],
            device_id={"boxyz": dest_of(s)})

    def fwd_copy(s):
        return pltpu.make_async_remote_copy(
            rcv.at[s], fwd.at[s], w_s.at[s], w_r.at[s], device_id={"boxx": partner})

    def own_basis(y, carry):
        for z in range(bzd):
            info = meta[y, z]
            count = info[:, face:]
            wide = jnp.concatenate([count, count], axis=1)
            rest = jnp.where(iota((16, face), 1) >= wide, F32(1.0), F32(0.0)).astype(BF)
            frame = jnp.concatenate([framed(pk[y, z], count), rest], axis=0)
            both = dot_t(frame, one_hot(info[:, :face], face))
            bas[y, z] = both[:smax].astype(BF)
            red[y, z] = both[smax:smax + 1]
        return carry

    early = by // 4
    lax.fori_loop(0, early, own_basis, 0)
    pl.semaphore_wait(barrier, near + 1 + jnp.where(has_far, 1, 0))
    rounds = steps_between(nyz, moves) - 1

    @pl.when(me > 0)
    def _():
        mz_copy().start()
        z_copy().start()

    @pl.when(has_far)
    def _():
        of_copy().start()
        mf_copy().start()

    greet(relay.at[0])
    for k in (1, 2):
        small(k).wait()
    lax.fori_loop(0, nyz, arrange, 0)
    pp_copy().start()
    lax.fori_loop(early, by, own_basis, 0)

    def stage_partner(s):
        g = ord_o[s]
        for c in range(4):
            y, z = child(g, c)
            stp[s, c] = bas[y, z]
        par_copy(s).start()

    def stage_far(s):
        g, _ = search(owner_f, s)
        for c in range(4):
            y, z = child(g, c)
            stf[s, c] = pk[y, z]
        far_copy(s).start()

    stage_partner(0)

    @pl.when(has_far)
    def _():
        of_copy().wait_recv()
        stage_far(0)
        stage_far(1)

    for k in range(1, rounds):
        pl.semaphore_wait(relay.at[k - 1], near)
        greet(relay.at[k])
    stage_partner(1)

    for y in range(by):
        for z in range(bzd):
            piv[y, z] = pv_v[y, z:z + 1, :]

    def received(packed, info):
        return dot_t(framed(packed, info[:, face:]), one_hot(info[:, :face], face)).astype(BF)

    @pl.when(me == last)
    def _():
        meta_z[...] = jnp.zeros_like(meta_z)

    @pl.when(me < last)
    def _():
        mz_copy().wait_recv()
        z_copy().wait_recv()

    for y in range(by):
        bas[y, bzd] = received(ze[y], meta_z[y])

    @pl.when(has_far)
    def _():
        mf_copy().wait_recv()

    def loaded(k):
        for y in range(by):
            load(k, y).wait()

    def base_half(s):
        g = ord_o[s]
        slot = lax.rem(s, 2)
        bases = []
        for c in range(4):
            y, z = child(g, c)
            basis = bas[y, z]
            proj = dot_t(basis, fb_v[y, z]).astype(BF)
            sk1[slot, c] = dot_t(basis, proj)
            bases.append(proj.astype(F32) + dot_t(bas[y, z + 1], cu_v[y, z]))
        return bases

    def first_half(s):
        g = ord_o[s]
        bases = base_half(s)
        for c in range(4):
            y, z = child(g, c)
            acc[lax.rem(s, 2), c] = bases[c] + dot_t(par[s, c], co_v[1, y, z])

    def far_basis(s, c):
        y, z = child(ord_o[s], c)
        return received(far[s, c], meta_f[y, z])

    def finish(s, c, y, z, total):
        coupling = red[y, z] * total
        scaled = (coupling * piv[y, z]).astype(BF)
        skl[s, c] = (sk1[lax.rem(s, 2), c] - dot_t(coupling.astype(BF), scaled)).astype(BF)

    def second_half(s, with_far):
        g = ord_o[s]
        slot = lax.rem(s, 2)
        for c in range(4):
            y, z = child(g, c)
            total = acc[slot, c]
            if with_far:
                total = total + dot_t(far_basis(s, c), co_v[0, y, z])
            finish(s, c, y, z, total)

    def send_pos(s, carry):
        pos_copy(s).start()
        return carry

    def all_groups(with_far):
        def arrive(s):
            if with_far:
                far_copy(s).wait_recv()

        def stage(s):
            stage_partner(s)
            if with_far:
                stage_far(s)

        start = jnp.int32(0)
        loaded(0)
        loaded(1)
        arrive(0)
        for c, base in enumerate(base_half(start)):
            acc[0, c] = base
            if with_far:
                fbas[c] = far_basis(start, c)
        par_copy(0).wait_recv()
        loaded(2)
        loaded(3)
        for c in range(4):
            y, z = child(ord_o[0], c)
            total = acc[0, c] + dot_t(par[0, c], co_v[1, y, z])
            if with_far:
                total = total + dot_t(fbas[c], co_v[0, y, z])
            finish(start, c, y, z, total)
        for k in range(rounds - 1, rounds):
            pl.semaphore_wait(relay.at[k], near)
        out_copy(0).start()
        stage(2)
        pp_copy().wait_recv()
        lax.fori_loop(0, last, send_pos, 0)
        par_copy(1).wait_recv()
        first_half(jnp.int32(1))

        def step(s, carry):
            @pl.when(s + 2 < nyz)
            def _():
                stage(s + 2)

            par_copy(s + 1).wait_recv()
            arrive(s)
            second_half(s, with_far)
            first_half(s + 1)
            out_copy(s).start()
            return carry

        lax.fori_loop(1, last, step, 0)
        arrive(last)
        second_half(jnp.int32(last), with_far)

    @pl.when(has_far)
    def _():
        all_groups(True)

    @pl.when(jnp.logical_not(has_far))
    def _():
        all_groups(False)

    rcv[last] = skl[last]
    posr[:, last] = posb[:, last]

    def expand(blocks, places):
        spots = [one_hot(places[c], PF) for c in range(4)]
        lifts = [dot(one_hot(places[c] - parity * rows, rows), blocks[c]).astype(BF)
                 for c in range(4)]
        return dot_t(jnp.concatenate(lifts, axis=1), jnp.concatenate(spots, axis=1)).astype(BF)

    def arrived(s):
        out_copy(s).wait_recv()
        pos_copy(s).wait_recv()
        fwd_copy(s).start()

    def own_side(s):
        half[s] = expand([rcv[s, c] for c in range(4)], [posr[0, s, c] for c in range(4)])

    def partner_side(s):
        value = expand([fwd[s, c] for c in range(4)], [posr[1, s, c] for c in range(4)])
        out[dest_of(s)] = (half[s].astype(F32) + value.astype(F32)).astype(BF)

    fwd_copy(last).start()
    own_side(last)
    arrived(0)
    own_side(0)
    fwd_copy(last).wait_recv()
    partner_side(last)

    def merge(s, carry):
        arrived(s)
        fwd_copy(s - 1).wait_recv()
        own_side(s)
        partner_side(s - 1)
        return carry

    lax.fori_loop(1, last, merge, 0)
    fwd_copy(last - 1).wait_recv()
    partner_side(last - 1)

    @pl.when(me > 0)
    def _():
        z_copy().wait_send()
        mz_copy().wait_send()

    @pl.when(has_far)
    def _():
        of_copy().wait_send()
        mf_copy().wait_send()
        for s in range(nyz):
            far_copy(s).wait_send()

    pp_copy().wait_send()
    for s in range(nyz):
        par_copy(s).wait_send()
        fwd_copy(s).wait_send()
    for s in range(last):
        out_copy(s).wait_send()
        pos_copy(s).wait_send()


def shards(nx, nyz, face_block, couple_minus, couple_plus, couple_up, interp, pivot_inv,
           face_order, skel_count, child_pos, owner):
    _, by, bzd, face, smax = interp.shape
    rows = PF // 2
    any_ = pl.BlockSpec(memory_space=pl.ANY)
    vmem = pl.BlockSpec(memory_space=pltpu.VMEM)
    smem = pl.BlockSpec(memory_space=pltpu.SMEM)
    dma = pltpu.SemaphoreType.DMA
    small = (smax, smax)
    rounds = steps_between(nyz, near_moves(nyz)) - 1
    out = pl.pallas_call(
        functools.partial(kernel, nx, nyz, by, bzd),
        name="eliminate",
        out_shape=pltpu.VMEM((nyz, rows, PF), BF),
        in_specs=[any_] * 6 + [smem, any_, any_, smem],
        out_specs=vmem,
        scratch_shapes=[pltpu.VMEM((by, bzd, face, face), BF)] * 2
        + [pltpu.VMEM((2, by, bzd, face, face), BF)]
        + [pltpu.VMEM((by, bzd, face, smax), BF)]
        + [pltpu.VMEM((by, bzd, face), I32), pltpu.VMEM((by, bzd, face), F32)]
        + [pltpu.VMEM((by, bzd, 1, smax), I32)]
        + [pltpu.VMEM((by, bzd) + small, BF)]
        + [pltpu.VMEM((nyz, 4) + small, BF)] * 2
        + [pltpu.VMEM((by,) + small, BF)]
        + [pltpu.VMEM((by, bzd, 1, face + smax), I32)] * 2
        + [pltpu.VMEM((by, 1, face + smax), I32)]
        + [pltpu.VMEM((by, bzd, 1, face), F32)] * 2
        + [pltpu.VMEM((by, bzd + 1, smax, face), BF)]
        + [pltpu.VMEM((nyz, 4, smax, face), BF)] * 2
        + [pltpu.VMEM((2, 4, smax, face), F32)]
        + [pltpu.VMEM((2, 4) + small, F32)]
        + [pltpu.VMEM((nyz, 4) + small, BF)] * 3
        + [pltpu.VMEM((2, nyz, 4, 1, smax), I32)] * 2
        + [pltpu.VMEM((nyz, rows, PF), BF)]
        + [pltpu.VMEM((4, smax, face), BF)]
        + [pltpu.SMEM((by // 2, bzd // 2), I32)]
        + [pltpu.SMEM((nyz,), I32)] * 2
        + [dma((4 * by,)), dma((by,)), dma((3,))]
        + [dma] * 10
        + [dma((nyz,))] * 10
        + [pltpu.SemaphoreType.REGULAR((rounds,))],
        compiler_params=pltpu.CompilerParams(
            collective_id=0, has_side_effects=True, vmem_limit_bytes=58 << 20),
    )(face_block[0], couple_minus[0], couple_plus[0], couple_up[0], interp[0],
      face_order[0], skel_count[0], pivot_inv[0],
      child_pos.reshape(by, bzd, 1, smax), owner[0].reshape(by // 2, bzd // 2))
    return out.reshape(1, nyz, 1, rows, PF)


def solution(mesh):
    return jax.shard_map(
        functools.partial(shards, mesh.shape["boxx"], mesh.shape["boxyz"]),
        mesh=mesh,
        in_specs=(P("boxx", None, "boxyz", None, None),) * 5
        + (P("boxx", None, "boxyz", None),) * 2
        + (P("boxx", None, "boxyz"), P("boxx", None, "boxyz", None), P("boxx", None, "boxyz")),
        out_specs=P("boxx", "boxyz", None, None, None),
        check_vma=False,
    )
```

```python
import functools

import jax
import jax.numpy as jnp
from jax import lax
from jax.experimental import pallas as pl
from jax.experimental.pallas import tpu as pltpu
from jax.sharding import PartitionSpec as P

PF = 384
BF = jnp.bfloat16
F32 = jnp.float32
I32 = jnp.int32


def iota(shape, dim):
    return lax.broadcasted_iota(I32, shape, dim)


def dot(a, b):
    return jnp.dot(a, b, preferred_element_type=F32)


def dot_t(a, b):
    return lax.dot_general(a, b, (((1,), (1,)), ((), ())), preferred_element_type=F32)


def framed(packed, count):
    n = packed.shape[0]
    row, col = iota((n, n), 0), iota((n, n), 1)
    zero = jnp.zeros((n, n), F32)
    live = row < count
    left = jnp.where(live & (col >= count), packed.astype(F32).T, zero)
    left = jnp.where(live & (row == col), F32(1.0) + left, left)
    right = jnp.where(live, packed.astype(F32), zero)
    return jnp.concatenate([left, right], axis=1).astype(BF)


def one_hot(order, size):
    return jnp.where(order == iota((size, order.shape[1]), 0), F32(1.0), F32(0.0)).astype(BF)


def steps_between(n, moves):
    worst = 0
    for start in range(n):
        seen, edge, far = {start}, {start}, 0
        while len(seen) < n:
            edge = {p + m for p in edge for m in moves if 0 <= p + m < n} - seen
            seen |= edge
            far += 1
        worst = max(worst, far)
    return worst


def near_moves(nyz):
    wide = 1 << ((nyz.bit_length() - 1) // 2)
    return tuple(sorted({1, -1, wide, -wide}))


def kernel(nx, nyz, by, bzd, fb, cm, cp, cu, interp, face_order, counts, pivots, pos, owner,
           out,
           fb_v, cu_v, co_v, ip_v, fo_v, pv_v, ps_v, pk, stf, far, ze, meta, meta_f, meta_z, red, bas,
           stp, par, acc, sk1, skl, rcv, fwd, posb, posp, posc, posr, half, fbas, mixed, swap, owner_f, ord_o, ord_f,
           in_sem, ip_sem, small_sem, sw_s, sw_r, wh_s, wh_r, z_s, z_r, mz_s, mz_r, mf_s, mf_r, of_s, of_r, pp_s, pp_r,
           p_s, p_r, f_s, f_r, o_s, o_r, po_s, po_r, w_s, w_r, relay):
    face, smax = interp.shape[2:]
    rows = out.shape[1]
    x = lax.axis_index("boxx")
    me = lax.axis_index("boxyz")
    parity = lax.rem(x, 2)
    partner = x + 1 - 2 * parity
    other = x - 1 + 2 * parity
    has_far = (other >= 0) & (other < nx)
    middle = nyz // 2
    last = nyz - 1
    groups_z = bzd // 2
    groups = (by // 2) * groups_z
    moves = near_moves(nyz)

    def small(k):
        src, dst = ((face_order, fo_v), (pivots, pv_v), (pos, ps_v))[k]
        return pltpu.make_async_copy(src, dst, small_sem.at[k])

    def interp_copy(y):
        return pltpu.make_async_copy(interp.at[y], ip_v.at[y], ip_sem.at[y])

    big = ((fb, fb_v), (cu, cu_v), (cm, co_v.at[parity]), (cp, co_v.at[1 - parity]))

    def load(k, y):
        return pltpu.make_async_copy(big[k][0].at[y], big[k][1].at[y], in_sem.at[k * by + y])

    small(0).start()
    for y in range(by):
        interp_copy(y).start()
    for k in (1, 2):
        small(k).start()

    barrier = pltpu.get_barrier_semaphore()
    pl.semaphore_signal(barrier, inc=1, device_id={"boxx": partner})

    @pl.when(has_far)
    def _():
        pl.semaphore_signal(barrier, inc=1, device_id={"boxx": other})

    def there(m):
        return (me + m >= 0) & (me + m < nyz)

    def greet(sem):
        for m in moves:
            @pl.when(there(m))
            def _(m=m):
                pl.semaphore_signal(sem, inc=1, device_id={"boxyz": me + m})

    near = jnp.int32(0)
    for m in moves:
        near = near + jnp.where(there(m), 1, 0)
    greet(barrier)

    def dest_of(s):
        mask = jnp.where(lax.rem(s, 2) == 0, middle, 0) + lax.rem(lax.div(s + 1, 2), middle)
        dest, bit = jnp.int32(0), 1
        while bit < nyz:
            mine, flip = lax.rem(lax.div(me, bit), 2), lax.rem(lax.div(mask, bit), 2)
            dest = dest + bit * (mine + flip - 2 * mine * flip)
            bit *= 2
        return dest

    def search(table, s):
        dest = dest_of(s)
        g, valid = jnp.int32(0), jnp.int32(0)
        for h in range(groups):
            hit = table[h // groups_z, h % groups_z] == dest
            g, valid = jnp.where(hit, h, g), jnp.where(hit, 1, valid)
        return g, valid

    def child(g, c):
        return 2 * lax.div(g, groups_z) + c // 2, 2 * lax.rem(g, groups_z) + c % 2

    small(0).wait()
    for y in range(by):
        for z in range(bzd):
            meta[y, z, :, :face] = fo_v[y, z:z + 1, :]
            meta[y, z, :, face:] = jnp.full((1, smax), counts[y, z], I32)

    def pack(y):
        for z in range(bzd):
            block = ip_v[y, z]
            count = meta[y, z][:, face:]
            bottom = block[smax:].astype(F32).T
            pk[y, z] = jnp.where(
                iota((smax, smax), 0) < count, bottom, block[:smax].astype(F32)).astype(BF)

    order = [[k for k in range(4) if min(k, by - 1) == y] for y in range(by)]
    for y in range(by):
        interp_copy(y).wait()
        for k in order[y]:
            for part in range(by):
                load(k, part).start()
        pack(y)

    def arrange(s, carry):
        g, valid = search(owner, s)
        ord_o[s] = g
        for c in range(4):
            y, z = child(g, c)
            posb[s, c:c + 1, :] = jnp.where(valid > 0, ps_v[y, z], -1)
        return carry

    def z_copy():
        return pltpu.make_async_remote_copy(
            pk.at[:, 0], ze, z_s, z_r, device_id={"boxyz": me - 1})

    def mz_copy():
        return pltpu.make_async_remote_copy(
            meta.at[:, 0], meta_z, mz_s, mz_r, device_id={"boxyz": me - 1})

    def mf_copy():
        return pltpu.make_async_remote_copy(
            meta, meta_f, mf_s, mf_r, device_id={"boxx": other})

    def of_copy():
        return pltpu.make_async_remote_copy(
            owner, owner_f, of_s, of_r, device_id={"boxx": other})

    def pp_copy():
        return pltpu.make_async_remote_copy(
            posb, posp, pp_s, pp_r, device_id={"boxx": partner})

    def par_copy(s):
        return pltpu.make_async_remote_copy(
            stp.at[s], par.at[s], p_s.at[s], p_r.at[s], device_id={"boxx": partner})

    def far_copy(s):
        return pltpu.make_async_remote_copy(
            stf.at[s], far.at[s], f_s.at[s], f_r.at[s], device_id={"boxx": other})

    def out_copy(s):
        return pltpu.make_async_remote_copy(
            skl.at[s], rcv.at[s], o_s.at[s], o_r.at[s], device_id={"boxyz": dest_of(s)})

    def pos_copy(s):
        return pltpu.make_async_remote_copy(
            posc.at[s], posr.at[s], po_s.at[s], po_r.at[s],
            device_id={"boxyz": dest_of(s)})

    def swap_copy():
        return pltpu.make_async_remote_copy(
            skl.at[last - 1], swap, sw_s, sw_r, device_id={"boxx": partner})

    def whole_copy():
        return pltpu.make_async_remote_copy(
            mixed, out.at[me], wh_s, wh_r, device_id={"boxyz": dest_of(last - 1)})

    def fwd_copy(s):
        return pltpu.make_async_remote_copy(
            rcv.at[s], fwd.at[s], w_s.at[s], w_r.at[s], device_id={"boxx": partner})

    def own_basis(y, carry):
        for z in range(bzd):
            info = meta[y, z]
            count = info[:, face:]
            wide = jnp.concatenate([count, count], axis=1)
            rest = jnp.where(iota((16, face), 1) >= wide, F32(1.0), F32(0.0)).astype(BF)
            frame = jnp.concatenate([framed(pk[y, z], count), rest], axis=0)
            both = dot_t(frame, one_hot(info[:, :face], face))
            bas[y, z] = both[:smax].astype(BF)
            red[y, z] = both[smax:smax + 1]
        return carry

    early = by // 4
    lax.fori_loop(0, early, own_basis, 0)
    pl.semaphore_wait(barrier, near + 1 + jnp.where(has_far, 1, 0))
    rounds = steps_between(nyz, moves) - 1

    @pl.when(me > 0)
    def _():
        mz_copy().start()
        z_copy().start()

    @pl.when(has_far)
    def _():
        of_copy().start()
        mf_copy().start()

    greet(relay.at[0])
    for k in (1, 2):
        small(k).wait()
    posb[...] = jnp.zeros_like(posb)
    lax.fori_loop(0, nyz, arrange, 0)
    pp_copy().start()
    lax.fori_loop(early, by, own_basis, 0)

    def stage_partner(s):
        g = ord_o[s]
        for c in range(4):
            y, z = child(g, c)
            stp[s, c] = bas[y, z]
        par_copy(s).start()

    def stage_far(s):
        g, _ = search(owner_f, s)
        for c in range(4):
            y, z = child(g, c)
            stf[s, c] = pk[y, z]
        far_copy(s).start()

    stage_partner(0)

    @pl.when(has_far)
    def _():
        of_copy().wait_recv()
        stage_far(0)
        stage_far(1)

    for k in range(1, rounds):
        pl.semaphore_wait(relay.at[k - 1], near)
        greet(relay.at[k])
    stage_partner(1)

    def received(packed, info):
        return dot_t(framed(packed, info[:, face:]), one_hot(info[:, :face], face)).astype(BF)

    @pl.when(me == last)
    def _():
        meta_z[...] = jnp.zeros_like(meta_z)

    @pl.when(me < last)
    def _():
        mz_copy().wait_recv()
        z_copy().wait_recv()

    for y in range(by):
        bas[y, bzd] = received(ze[y], meta_z[y])

    @pl.when(has_far)
    def _():
        mf_copy().wait_recv()

    def loaded(k):
        for y in range(by):
            load(k, y).wait()

    def base_half(s):
        g = ord_o[s]
        slot = lax.rem(s, 2)
        bases = []
        for c in range(4):
            y, z = child(g, c)
            basis = bas[y, z]
            proj = dot_t(basis, fb_v[y, z]).astype(BF)
            sk1[slot, c] = dot_t(basis, proj)
            bases.append(proj.astype(F32) + dot_t(bas[y, z + 1], cu_v[y, z]))
        return bases

    def first_half(s):
        g = ord_o[s]
        bases = base_half(s)
        for c in range(4):
            y, z = child(g, c)
            acc[lax.rem(s, 2), c] = bases[c] + dot_t(par[s, c], co_v[1, y, z])

    def far_basis(s, c):
        y, z = child(ord_o[s], c)
        return received(far[s, c], meta_f[y, z])

    def finish(s, c, y, z, total):
        coupling = red[y, z] * total
        scaled = (coupling * pv_v[y, pl.ds(z, 1), :]).astype(BF)
        skl[s, c] = (sk1[lax.rem(s, 2), c] - dot_t(coupling.astype(BF), scaled)).astype(BF)

    def second_half(s, with_far):
        g = ord_o[s]
        slot = lax.rem(s, 2)
        for c in range(4):
            y, z = child(g, c)
            total = acc[slot, c]
            if with_far:
                total = total + dot_t(far_basis(s, c), co_v[0, y, z])
            finish(s, c, y, z, total)

    def places(table, s, first):
        return [table[s, first + c:first + c + 1, :] for c in range(4)]

    def expand(blocks, where):
        spots = [one_hot(where[c], PF) for c in range(4)]
        lifts = [dot(one_hot(where[c] - parity * rows, rows), blocks[c]).astype(BF)
                 for c in range(4)]
        return dot_t(jnp.concatenate(lifts, axis=1), jnp.concatenate(spots, axis=1)).astype(BF)

    def send_pos(s, carry):
        pos_copy(s).start()
        return carry

    def all_groups(with_far):
        def arrive(s):
            if with_far:
                far_copy(s).wait_recv()

        def stage(s):
            stage_partner(s)
            if with_far:
                stage_far(s)

        start = jnp.int32(0)
        loaded(0)
        loaded(1)
        arrive(0)
        for c, base in enumerate(base_half(start)):
            acc[0, c] = base
            if with_far:
                fbas[c] = far_basis(start, c)
        par_copy(0).wait_recv()
        loaded(2)
        loaded(3)
        for c in range(4):
            y, z = child(ord_o[0], c)
            total = acc[0, c] + dot_t(par[0, c], co_v[1, y, z])
            if with_far:
                total = total + dot_t(fbas[c], co_v[0, y, z])
            finish(start, c, y, z, total)
        for k in range(rounds - 1, rounds):
            pl.semaphore_wait(relay.at[k], near)
        out_copy(0).start()
        stage(2)
        pp_copy().wait_recv()
        for k in range(nyz):
            posc[k] = jnp.concatenate([posb[k, :4], posp[k, :4]], axis=0)
        lax.fori_loop(0, last - 1, send_pos, 0)
        par_copy(1).wait_recv()
        first_half(jnp.int32(1))

        def step(s, carry):
            @pl.when(s + 2 < nyz)
            def _():
                stage(s + 2)

            par_copy(s + 1).wait_recv()
            arrive(s)
            second_half(s, with_far)
            first_half(s + 1)

            @pl.when(s < last - 1)
            def _():
                out_copy(s).start()

            @pl.when(s == last - 1)
            def _():
                swap_copy().start()

            return carry

        lax.fori_loop(1, last, step, 0)
        arrive(last)
        second_half(jnp.int32(last), with_far)

    @pl.when(has_far)
    def _():
        all_groups(True)

    @pl.when(jnp.logical_not(has_far))
    def _():
        all_groups(False)

    swap_copy().wait_recv()
    mine = expand([skl[last - 1, c] for c in range(4)], places(posc, last - 1, 0))
    theirs = expand([swap[c] for c in range(4)], places(posc, last - 1, 4))
    mixed[...] = (mine.astype(F32) + theirs.astype(F32)).astype(BF)
    whole_copy().start()

    rcv[last] = skl[last]
    posr[last] = posc[last]

    def arrived(s):
        out_copy(s).wait_recv()
        pos_copy(s).wait_recv()
        fwd_copy(s).start()

    def own_side(s):
        half[s] = expand([rcv[s, c] for c in range(4)], places(posr, s, 0))

    def partner_side(s):
        value = expand([fwd[s, c] for c in range(4)], places(posr, s, 4))
        out[dest_of(s)] = (half[s].astype(F32) + value.astype(F32)).astype(BF)

    fwd_copy(last).start()
    own_side(last)
    arrived(0)
    own_side(0)
    fwd_copy(last).wait_recv()
    partner_side(last)

    def merge(s, carry):
        arrived(s)
        fwd_copy(s - 1).wait_recv()
        own_side(s)
        partner_side(s - 1)
        return carry

    lax.fori_loop(1, last - 1, merge, 0)
    fwd_copy(last - 2).wait_recv()
    partner_side(last - 2)
    whole_copy().wait()

    @pl.when(me > 0)
    def _():
        z_copy().wait_send()
        mz_copy().wait_send()

    @pl.when(has_far)
    def _():
        of_copy().wait_send()
        mf_copy().wait_send()
        for s in range(nyz):
            far_copy(s).wait_send()

    pp_copy().wait_send()
    swap_copy().wait_send()
    fwd_copy(last).wait_send()
    for s in range(nyz):
        par_copy(s).wait_send()
    for s in range(last - 1):
        fwd_copy(s).wait_send()
        out_copy(s).wait_send()
        pos_copy(s).wait_send()


def shards(nx, nyz, face_block, couple_minus, couple_plus, couple_up, interp, pivot_inv,
           face_order, skel_count, child_pos, owner):
    _, by, bzd, face, smax = interp.shape
    rows = PF // 2
    any_ = pl.BlockSpec(memory_space=pl.ANY)
    vmem = pl.BlockSpec(memory_space=pltpu.VMEM)
    smem = pl.BlockSpec(memory_space=pltpu.SMEM)
    dma = pltpu.SemaphoreType.DMA
    small = (smax, smax)
    rounds = steps_between(nyz, near_moves(nyz)) - 1
    out = pl.pallas_call(
        functools.partial(kernel, nx, nyz, by, bzd),
        name="eliminate",
        out_shape=pltpu.VMEM((nyz, rows, PF), BF),
        in_specs=[any_] * 6 + [smem, any_, any_, smem],
        out_specs=vmem,
        scratch_shapes=[pltpu.VMEM((by, bzd, face, face), BF)] * 2
        + [pltpu.VMEM((2, by, bzd, face, face), BF)]
        + [pltpu.VMEM((by, bzd, face, smax), BF)]
        + [pltpu.VMEM((by, bzd, face), I32), pltpu.VMEM((by, bzd, face), F32)]
        + [pltpu.VMEM((by, bzd, 1, smax), I32)]
        + [pltpu.VMEM((by, bzd) + small, BF)]
        + [pltpu.VMEM((nyz, 4) + small, BF)] * 2
        + [pltpu.VMEM((by,) + small, BF)]
        + [pltpu.VMEM((by, bzd, 1, face + smax), I32)] * 2
        + [pltpu.VMEM((by, 1, face + smax), I32)]
        + [pltpu.VMEM((by, bzd, 1, face), F32)]
        + [pltpu.VMEM((by, bzd + 1, smax, face), BF)]
        + [pltpu.VMEM((nyz, 4, smax, face), BF)] * 2
        + [pltpu.VMEM((2, 4, smax, face), F32)]
        + [pltpu.VMEM((2, 4) + small, F32)]
        + [pltpu.VMEM((nyz, 4) + small, BF)] * 3
        + [pltpu.VMEM((nyz, 8, smax), I32)] * 4
        + [pltpu.VMEM((nyz, rows, PF), BF)]
        + [pltpu.VMEM((4, smax, face), BF)]
        + [pltpu.VMEM((rows, PF), BF)]
        + [pltpu.VMEM((4,) + small, BF)]
        + [pltpu.SMEM((by // 2, bzd // 2), I32)]
        + [pltpu.SMEM((nyz,), I32)] * 2
        + [dma((4 * by,)), dma((by,)), dma((3,))]
        + [dma] * 14
        + [dma((nyz,))] * 10
        + [pltpu.SemaphoreType.REGULAR((rounds,))],
        compiler_params=pltpu.CompilerParams(
            collective_id=0, has_side_effects=True, vmem_limit_bytes=58 << 20),
    )(face_block[0], couple_minus[0], couple_plus[0], couple_up[0], interp[0],
      face_order[0], skel_count[0], pivot_inv[0],
      child_pos.reshape(by, bzd, 1, smax), owner[0].reshape(by // 2, bzd // 2))
    return out.reshape(1, nyz, 1, rows, PF)


def solution(mesh):
    return jax.shard_map(
        functools.partial(shards, mesh.shape["boxx"], mesh.shape["boxyz"]),
        mesh=mesh,
        in_specs=(P("boxx", None, "boxyz", None, None),) * 5
        + (P("boxx", None, "boxyz", None),) * 2
        + (P("boxx", None, "boxyz"), P("boxx", None, "boxyz", None), P("boxx", None, "boxyz")),
        out_specs=P("boxx", "boxyz", None, None, None),
        check_vma=False,
    )
```

```python
import functools

import jax
import jax.numpy as jnp
from jax import lax
from jax.experimental import pallas as pl
from jax.experimental.pallas import tpu as pltpu
from jax.sharding import PartitionSpec as P

PF = 384
BF = jnp.bfloat16
F32 = jnp.float32
I32 = jnp.int32


def iota(shape, dim):
    return lax.broadcasted_iota(I32, shape, dim)


def dot(a, b):
    return jnp.dot(a, b, preferred_element_type=F32)


def dot_t(a, b):
    return lax.dot_general(a, b, (((1,), (1,)), ((), ())), preferred_element_type=F32)


def framed(packed, count):
    n = packed.shape[0]
    row, col = iota((n, n), 0), iota((n, n), 1)
    zero = jnp.zeros((n, n), F32)
    live = row < count
    left = jnp.where(live & (col >= count), packed.astype(F32).T, zero)
    left = jnp.where(live & (row == col), F32(1.0) + left, left)
    right = jnp.where(live, packed.astype(F32), zero)
    return jnp.concatenate([left, right], axis=1).astype(BF)


def one_hot(order, size):
    return jnp.where(order == iota((size, order.shape[1]), 0), F32(1.0), F32(0.0)).astype(BF)


def steps_between(n, moves):
    worst = 0
    for start in range(n):
        seen, edge, far = {start}, {start}, 0
        while len(seen) < n:
            edge = {p + m for p in edge for m in moves if 0 <= p + m < n} - seen
            seen |= edge
            far += 1
        worst = max(worst, far)
    return worst


def near_moves(nyz):
    wide = 1 << ((nyz.bit_length() - 1) // 2)
    return tuple(sorted({1, -1, wide, -wide}))


def kernel(nx, nyz, by, bzd, fb, cm, cp, cu, interp, face_order, counts, pivots, pos, owner,
           out,
           fb_v, cu_v, co_v, ip_v, fo_v, pv_v, ps_v, pk, stf, far, ze, meta, meta_f, meta_z, red, bas,
           stp, par, acc, sk1, skl, rcv, fwd, posb, posp, posc, posr, half, fbas, mixed, swap, owner_f, ord_o, ord_f,
           in_sem, ip_sem, small_sem, sw_s, sw_r, wh_s, wh_r, z_s, z_r, mz_s, mz_r, mf_s, mf_r, of_s, of_r, pp_s, pp_r,
           p_s, p_r, f_s, f_r, o_s, o_r, po_s, po_r, w_s, w_r, relay):
    face, smax = interp.shape[2:]
    rows = out.shape[1]
    x = lax.axis_index("boxx")
    me = lax.axis_index("boxyz")
    parity = lax.rem(x, 2)
    partner = x + 1 - 2 * parity
    other = x - 1 + 2 * parity
    has_far = (other >= 0) & (other < nx)
    middle = nyz // 2
    last = nyz - 1
    groups_z = bzd // 2
    groups = (by // 2) * groups_z
    moves = near_moves(nyz)

    def small(k):
        src, dst = ((face_order, fo_v), (pivots, pv_v), (pos, ps_v))[k]
        return pltpu.make_async_copy(src, dst, small_sem.at[k])

    def interp_copy(y):
        return pltpu.make_async_copy(interp.at[y], ip_v.at[y], ip_sem.at[y])

    big = ((fb, fb_v), (cu, cu_v), (cm, co_v.at[parity]), (cp, co_v.at[1 - parity]))

    def load(k, y):
        return pltpu.make_async_copy(big[k][0].at[y], big[k][1].at[y], in_sem.at[k * by + y])

    small(0).start()
    for y in range(by):
        interp_copy(y).start()
    for k in (1, 2):
        small(k).start()

    barrier = pltpu.get_barrier_semaphore()
    pl.semaphore_signal(barrier, inc=1, device_id={"boxx": partner})

    @pl.when(has_far)
    def _():
        pl.semaphore_signal(barrier, inc=1, device_id={"boxx": other})

    def there(m):
        return (me + m >= 0) & (me + m < nyz)

    def greet(sem):
        for m in moves:
            @pl.when(there(m))
            def _(m=m):
                pl.semaphore_signal(sem, inc=1, device_id={"boxyz": me + m})

    near = jnp.int32(0)
    for m in moves:
        near = near + jnp.where(there(m), 1, 0)
    greet(barrier)

    def dest_of(s):
        mask = jnp.where(lax.rem(s, 2) == 0, middle, 0) + lax.rem(lax.div(s + 1, 2), middle)
        dest, bit = jnp.int32(0), 1
        while bit < nyz:
            mine, flip = lax.rem(lax.div(me, bit), 2), lax.rem(lax.div(mask, bit), 2)
            dest = dest + bit * (mine + flip - 2 * mine * flip)
            bit *= 2
        return dest

    def search(table, s):
        dest = dest_of(s)
        g, valid = jnp.int32(0), jnp.int32(0)
        for h in range(groups):
            hit = table[h // groups_z, h % groups_z] == dest
            g, valid = jnp.where(hit, h, g), jnp.where(hit, 1, valid)
        return g, valid

    def child(g, c):
        return 2 * lax.div(g, groups_z) + c // 2, 2 * lax.rem(g, groups_z) + c % 2

    small(0).wait()
    def pack(y):
        for z in range(bzd):
            block = ip_v[y, z]
            count = meta[y, z][:, face:]
            bottom = block[smax:].astype(F32).T
            pk[y, z] = jnp.where(
                iota((smax, smax), 0) < count, bottom, block[:smax].astype(F32)).astype(BF)

    def take(y, carry):
        for z in range(bzd):
            meta[y, z, :, :face] = fo_v[y, z:z + 1, :]
            meta[y, z, :, face:] = jnp.full((1, smax), counts[y, z], I32)
        interp_copy(y).wait()
        for k in range(4):
            @pl.when(y == min(k, by - 1))
            def _(k=k):
                for part in range(by):
                    load(k, part).start()
        pack(y)
        return carry

    lax.fori_loop(0, by, take, 0)

    def arrange(s, carry):
        g, valid = search(owner, s)
        ord_o[s] = g
        for c in range(4):
            y, z = child(g, c)
            posb[s, c:c + 1, :] = jnp.where(valid > 0, ps_v[y, z], -1)
        return carry

    def z_copy():
        return pltpu.make_async_remote_copy(
            pk.at[:, 0], ze, z_s, z_r, device_id={"boxyz": me - 1})

    def mz_copy():
        return pltpu.make_async_remote_copy(
            meta.at[:, 0], meta_z, mz_s, mz_r, device_id={"boxyz": me - 1})

    def mf_copy():
        return pltpu.make_async_remote_copy(
            meta, meta_f, mf_s, mf_r, device_id={"boxx": other})

    def of_copy():
        return pltpu.make_async_remote_copy(
            owner, owner_f, of_s, of_r, device_id={"boxx": other})

    def pp_copy():
        return pltpu.make_async_remote_copy(
            posb, posp, pp_s, pp_r, device_id={"boxx": partner})

    def par_copy(s):
        return pltpu.make_async_remote_copy(
            stp.at[s], par.at[s], p_s.at[s], p_r.at[s], device_id={"boxx": partner})

    def far_copy(s):
        return pltpu.make_async_remote_copy(
            stf.at[s], far.at[s], f_s.at[s], f_r.at[s], device_id={"boxx": other})

    def out_copy(s):
        return pltpu.make_async_remote_copy(
            skl.at[s], rcv.at[s], o_s.at[s], o_r.at[s], device_id={"boxyz": dest_of(s)})

    def pos_copy(s):
        return pltpu.make_async_remote_copy(
            posc.at[s], posr.at[s], po_s.at[s], po_r.at[s],
            device_id={"boxyz": dest_of(s)})

    def swap_copy():
        return pltpu.make_async_remote_copy(
            skl.at[last - 1], swap, sw_s, sw_r, device_id={"boxx": partner})

    def whole_copy():
        return pltpu.make_async_remote_copy(
            mixed, out.at[me], wh_s, wh_r, device_id={"boxyz": dest_of(last - 1)})

    def fwd_copy(s):
        return pltpu.make_async_remote_copy(
            rcv.at[s], fwd.at[s], w_s.at[s], w_r.at[s], device_id={"boxx": partner})

    def own_basis(y, carry):
        for z in range(bzd):
            info = meta[y, z]
            count = info[:, face:]
            wide = jnp.concatenate([count, count], axis=1)
            rest = jnp.where(iota((16, face), 1) >= wide, F32(1.0), F32(0.0)).astype(BF)
            frame = jnp.concatenate([framed(pk[y, z], count), rest], axis=0)
            both = dot_t(frame, one_hot(info[:, :face], face))
            bas[y, z] = both[:smax].astype(BF)
            red[y, z] = both[smax:smax + 1]
        return carry

    early = by // 4
    lax.fori_loop(0, early, own_basis, 0)
    pl.semaphore_wait(barrier, near + 1 + jnp.where(has_far, 1, 0))
    rounds = steps_between(nyz, moves) - 1

    @pl.when(me > 0)
    def _():
        mz_copy().start()
        z_copy().start()

    @pl.when(has_far)
    def _():
        of_copy().start()
        mf_copy().start()

    greet(relay.at[0])
    for k in (1, 2):
        small(k).wait()
    posb[...] = jnp.zeros_like(posb)
    lax.fori_loop(0, nyz, arrange, 0)
    pp_copy().start()
    lax.fori_loop(early, by, own_basis, 0)

    def stage_partner(s):
        g = ord_o[s]
        for c in range(4):
            y, z = child(g, c)
            stp[s, c] = bas[y, z]
        par_copy(s).start()

    def stage_far(s):
        g, _ = search(owner_f, s)
        for c in range(4):
            y, z = child(g, c)
            stf[s, c] = pk[y, z]
        far_copy(s).start()

    stage_partner(0)

    @pl.when(has_far)
    def _():
        of_copy().wait_recv()
        stage_far(0)
        stage_far(1)

    for k in range(1, rounds):
        pl.semaphore_wait(relay.at[k - 1], near)
        greet(relay.at[k])
    stage_partner(1)

    def received(packed, info):
        return dot_t(framed(packed, info[:, face:]), one_hot(info[:, :face], face)).astype(BF)

    @pl.when(me == last)
    def _():
        meta_z[...] = jnp.zeros_like(meta_z)

    @pl.when(me < last)
    def _():
        mz_copy().wait_recv()
        z_copy().wait_recv()

    for y in range(by):
        bas[y, bzd] = received(ze[y], meta_z[y])

    @pl.when(has_far)
    def _():
        mf_copy().wait_recv()

    def loaded(k):
        for y in range(by):
            load(k, y).wait()

    def base_half(s):
        g = ord_o[s]
        slot = lax.rem(s, 2)
        bases = []
        for c in range(4):
            y, z = child(g, c)
            basis = bas[y, z]
            proj = dot_t(basis, fb_v[y, z]).astype(BF)
            sk1[slot, c] = dot_t(basis, proj)
            bases.append(proj.astype(F32) + dot_t(bas[y, z + 1], cu_v[y, z]))
        return bases

    def first_half(s):
        g = ord_o[s]
        bases = base_half(s)
        for c in range(4):
            y, z = child(g, c)
            acc[lax.rem(s, 2), c] = bases[c] + dot_t(par[s, c], co_v[1, y, z])

    def far_basis(s, c):
        y, z = child(ord_o[s], c)
        return received(far[s, c], meta_f[y, z])

    def finish(s, c, y, z, total):
        coupling = red[y, z] * total
        scaled = (coupling * pv_v[y, pl.ds(z, 1), :]).astype(BF)
        skl[s, c] = (sk1[lax.rem(s, 2), c] - dot_t(coupling.astype(BF), scaled)).astype(BF)

    def second_half(s, with_far):
        g = ord_o[s]
        slot = lax.rem(s, 2)
        for c in range(4):
            y, z = child(g, c)
            total = acc[slot, c]
            if with_far:
                total = total + dot_t(far_basis(s, c), co_v[0, y, z])
            finish(s, c, y, z, total)

    def places(table, s, first):
        return [table[s, first + c:first + c + 1, :] for c in range(4)]

    def expand(blocks, where):
        spots = [one_hot(where[c], PF) for c in range(4)]
        lifts = [dot(one_hot(where[c] - parity * rows, rows), blocks[c]).astype(BF)
                 for c in range(4)]
        return dot_t(jnp.concatenate(lifts, axis=1), jnp.concatenate(spots, axis=1)).astype(BF)

    def send_pos(s, carry):
        pos_copy(s).start()
        return carry

    def all_groups(with_far):
        def arrive(s):
            if with_far:
                far_copy(s).wait_recv()

        def stage(s):
            stage_partner(s)
            if with_far:
                stage_far(s)

        start = jnp.int32(0)
        loaded(0)
        loaded(1)
        arrive(0)
        for c, base in enumerate(base_half(start)):
            acc[0, c] = base
            if with_far:
                fbas[c] = far_basis(start, c)
        par_copy(0).wait_recv()
        loaded(2)
        loaded(3)
        for c in range(4):
            y, z = child(ord_o[0], c)
            total = acc[0, c] + dot_t(par[0, c], co_v[1, y, z])
            if with_far:
                total = total + dot_t(fbas[c], co_v[0, y, z])
            finish(start, c, y, z, total)
        for k in range(rounds - 1, rounds):
            pl.semaphore_wait(relay.at[k], near)
        out_copy(0).start()
        stage(2)
        pp_copy().wait_recv()
        for k in range(nyz):
            posc[k] = jnp.concatenate([posb[k, :4], posp[k, :4]], axis=0)
        lax.fori_loop(0, last - 1, send_pos, 0)
        par_copy(1).wait_recv()
        first_half(jnp.int32(1))

        def step(s, carry):
            @pl.when(s + 2 < nyz)
            def _():
                stage(s + 2)

            par_copy(s + 1).wait_recv()
            arrive(s)
            second_half(s, with_far)
            first_half(s + 1)

            @pl.when(s < last - 1)
            def _():
                out_copy(s).start()

            @pl.when(s == last - 1)
            def _():
                swap_copy().start()

            return carry

        lax.fori_loop(1, last, step, 0)
        arrive(last)
        second_half(jnp.int32(last), with_far)

    @pl.when(has_far)
    def _():
        all_groups(True)

    @pl.when(jnp.logical_not(has_far))
    def _():
        all_groups(False)

    swap_copy().wait_recv()
    mine = expand([skl[last - 1, c] for c in range(4)], places(posc, last - 1, 0))
    theirs = expand([swap[c] for c in range(4)], places(posc, last - 1, 4))
    mixed[...] = (mine.astype(F32) + theirs.astype(F32)).astype(BF)
    whole_copy().start()

    rcv[last] = skl[last]
    posr[last] = posc[last]

    def arrived(s):
        out_copy(s).wait_recv()
        pos_copy(s).wait_recv()
        fwd_copy(s).start()

    def own_side(s):
        half[s] = expand([rcv[s, c] for c in range(4)], places(posr, s, 0))

    def partner_side(s):
        value = expand([fwd[s, c] for c in range(4)], places(posr, s, 4))
        out[dest_of(s)] = (half[s].astype(F32) + value.astype(F32)).astype(BF)

    fwd_copy(last).start()
    own_side(last)
    arrived(0)
    own_side(0)
    fwd_copy(last).wait_recv()
    partner_side(last)

    def merge(s, carry):
        arrived(s)
        fwd_copy(s - 1).wait_recv()
        own_side(s)
        partner_side(s - 1)
        return carry

    lax.fori_loop(1, last - 1, merge, 0)
    fwd_copy(last - 2).wait_recv()
    partner_side(last - 2)
    whole_copy().wait()

    @pl.when(me > 0)
    def _():
        z_copy().wait_send()
        mz_copy().wait_send()

    @pl.when(has_far)
    def _():
        of_copy().wait_send()
        mf_copy().wait_send()
        for s in range(nyz):
            far_copy(s).wait_send()

    pp_copy().wait_send()
    swap_copy().wait_send()
    fwd_copy(last).wait_send()
    for s in range(nyz):
        par_copy(s).wait_send()
    for s in range(last - 1):
        fwd_copy(s).wait_send()
        out_copy(s).wait_send()
        pos_copy(s).wait_send()


def shards(nx, nyz, face_block, couple_minus, couple_plus, couple_up, interp, pivot_inv,
           face_order, skel_count, child_pos, owner):
    _, by, bzd, face, smax = interp.shape
    rows = PF // 2
    any_ = pl.BlockSpec(memory_space=pl.ANY)
    vmem = pl.BlockSpec(memory_space=pltpu.VMEM)
    smem = pl.BlockSpec(memory_space=pltpu.SMEM)
    dma = pltpu.SemaphoreType.DMA
    small = (smax, smax)
    rounds = steps_between(nyz, near_moves(nyz)) - 1
    out = pl.pallas_call(
        functools.partial(kernel, nx, nyz, by, bzd),
        name="eliminate",
        out_shape=pltpu.VMEM((nyz, rows, PF), BF),
        in_specs=[any_] * 6 + [smem, any_, any_, smem],
        out_specs=vmem,
        scratch_shapes=[pltpu.VMEM((by, bzd, face, face), BF)] * 2
        + [pltpu.VMEM((2, by, bzd, face, face), BF)]
        + [pltpu.VMEM((by, bzd, face, smax), BF)]
        + [pltpu.VMEM((by, bzd, face), I32), pltpu.VMEM((by, bzd, face), F32)]
        + [pltpu.VMEM((by, bzd, 1, smax), I32)]
        + [pltpu.VMEM((by, bzd) + small, BF)]
        + [pltpu.VMEM((nyz, 4) + small, BF)] * 2
        + [pltpu.VMEM((by,) + small, BF)]
        + [pltpu.VMEM((by, bzd, 1, face + smax), I32)] * 2
        + [pltpu.VMEM((by, 1, face + smax), I32)]
        + [pltpu.VMEM((by, bzd, 1, face), F32)]
        + [pltpu.VMEM((by, bzd + 1, smax, face), BF)]
        + [pltpu.VMEM((nyz, 4, smax, face), BF)] * 2
        + [pltpu.VMEM((2, 4, smax, face), F32)]
        + [pltpu.VMEM((2, 4) + small, F32)]
        + [pltpu.VMEM((nyz, 4) + small, BF)] * 3
        + [pltpu.VMEM((nyz, 8, smax), I32)] * 4
        + [pltpu.VMEM((nyz, rows, PF), BF)]
        + [pltpu.VMEM((4, smax, face), BF)]
        + [pltpu.VMEM((rows, PF), BF)]
        + [pltpu.VMEM((4,) + small, BF)]
        + [pltpu.SMEM((by // 2, bzd // 2), I32)]
        + [pltpu.SMEM((nyz,), I32)] * 2
        + [dma((4 * by,)), dma((by,)), dma((3,))]
        + [dma] * 14
        + [dma((nyz,))] * 10
        + [pltpu.SemaphoreType.REGULAR((rounds,))],
        compiler_params=pltpu.CompilerParams(
            collective_id=0, has_side_effects=True, vmem_limit_bytes=58 << 20),
    )(face_block[0], couple_minus[0], couple_plus[0], couple_up[0], interp[0],
      face_order[0], skel_count[0], pivot_inv[0],
      child_pos.reshape(by, bzd, 1, smax), owner[0].reshape(by // 2, bzd // 2))
    return out.reshape(1, nyz, 1, rows, PF)


def solution(mesh):
    return jax.shard_map(
        functools.partial(shards, mesh.shape["boxx"], mesh.shape["boxyz"]),
        mesh=mesh,
        in_specs=(P("boxx", None, "boxyz", None, None),) * 5
        + (P("boxx", None, "boxyz", None),) * 2
        + (P("boxx", None, "boxyz"), P("boxx", None, "boxyz", None), P("boxx", None, "boxyz")),
        out_specs=P("boxx", "boxyz", None, None, None),
        check_vma=False,
    )
```
